32 devices in a mesh: tok: 16 (over z, y, x), hd: 2 (over core).
Axes of the slice: x: 2, y: 2, z: 4, core: 2. Of those that a mesh axis runs over, the one named last changes fastest.
Arguments:
- hidden_in: bfloat16 [16384, 768], P(('tok', 'hd')), may hold values from -6 to 6
- norm_gains: bfloat16 [2, 768], P(None, ('tok', 'hd')), may hold values from 0.099609375 to 1.8984375
- w_qkv: bfloat16 [2304, 768], P(('tok', 'hd')), may hold values from -0.21875 to 0.21875
- w_attn_out: bfloat16 [768, 768], P(('tok', 'hd')), may hold values from -1.75 to 1.75
- w_in: bfloat16 [2304, 768], P(('tok', 'hd')), may hold values from -0.21875 to 0.21875
- w_down: bfloat16 [768, 1152], P(('tok', 'hd')), may hold values from -0.1875 to 0.1875
- cotangent: bfloat16 [16384, 768], P(('tok', 'hd')), may hold values from -6 to 6
- segment_ids: int32 [16384], P(('tok', 'hd')), may hold values from 0 to 31, as said below
- row_counts: int32 [32], P(('tok', 'hd')), may hold values from 256 to 512, as said below
Outputs:
- output: bfloat16 [16384, 768], P(('tok', 'hd'))
- input_grad: bfloat16 [16384, 768], P(('tok', 'hd'))
- grad_qkv: float32 [2304, 768], P(('tok', 'hd'))
- grad_attn_out: float32 [768, 768], P(('tok', 'hd'))
- grad_in: float32 [2304, 768], P(('tok', 'hd'))
- grad_down: float32 [768, 1152], P(('tok', 'hd'))
- grad_gains: float32 [2, 768], P(None, ('tok', 'hd'))
The draws below stay inside these ranges and needn't reach their ends.
Inputs may be any that keep to these rules, and one draw needn't show every extreme that they name: `segment_ids`: within each group of 1024 rows the ids start at 0 and never fall; a document is a run of rows with one id; documents begin only at rows whose index within the group is a multiple of 32, and always at rows whose index within a block is 256, so a document may span two blocks of a group. In every draw some group holds 32 documents. `row_counts`: rows of a block at or beyond its count are padding.
All inputs are finite; a program needn't handle non-finite values.
Results may differ from the reference program's by a relative error of at most 0.015.
Values may be sent and summed in bfloat16 or wider, within the bound.
A program may use at most 192 MiB of HBM per device.

```python
import math
import jax
import jax.numpy as jnp
from jax import lax

D = 768
HEADS = 12
HEAD_DIM = 64
FF = 1152
TOK_DEV = 512
TOKENS = 16384
N_TOK = 16
N_HD = 2


def layout_draw(key):
    group_count = N_TOK
    group_rows = N_HD * TOK_DEV
    key_cut, key_count, key_full = jax.random.split(jax.random.fold_in(key, 7), 3)
    step_rows = TOK_DEV // 16
    row_index = jnp.arange(group_rows)
    on_grid = (row_index % step_rows == 0) & (row_index > 0)
    forced = row_index % TOK_DEV == TOK_DEV // 2
    coin = jax.random.randint(key_cut, (group_count, group_rows), 0, 4) == 0
    full_group = jax.random.randint(key_full, (), 0, group_count)
    many_group = (full_group + 1) % group_count
    group_index = jnp.arange(group_count)
    cuts = forced[None, :] | on_grid[None, :] & (coin | (group_index == many_group)[:, None])
    cuts = jnp.where((group_index == full_group)[:, None], forced[None, :], cuts)
    seg_ids = jnp.cumsum(cuts.astype(jnp.int32), axis=1).astype(jnp.int32)
    block_index = jnp.arange(group_count * N_HD)
    row_counts = jax.random.randint(key_count, (group_count * N_HD,), TOK_DEV // 2, TOK_DEV + 1)
    row_counts = jnp.where(block_index // N_HD == full_group, TOK_DEV, row_counts)
    row_counts = jnp.where(block_index == many_group * N_HD, TOK_DEV // 2, row_counts).astype(jnp.int32)
    return (seg_ids.reshape(-1), row_counts)


def draw_segment_ids(key, part):
    return layout_draw(key)[0]


def draw_row_counts(key, part):
    return layout_draw(key)[1]


def strengthened(values, own_key, source, target, parts, factor):
    def block_of(dim):
        return (jnp.arange(values.shape[dim]) // (values.shape[dim] // parts)).reshape((-1,) + (1,) * (values.ndim - 1 - dim))

    first = jax.random.permutation(own_key, parts)[block_of(target)]
    second = (block_of(target) + parts // 2) % parts
    return jnp.where((block_of(source) == first) | (block_of(source) == second), factor * values, values)


def block_levels(key, dims, cuts, smallest, high):
    def one(dim, parts):
        heights = jax.random.uniform(jax.random.fold_in(jax.random.fold_in(key, 6), dim), (parts,), jnp.float32, smallest / len(cuts), high / len(cuts))
        return jnp.repeat(jnp.exp(heights), dims[dim] // parts).reshape((-1,) + (1,) * (len(dims) - dim - 1))

    loudness = one(*cuts[0])
    for cut in cuts[1:]:
        loudness = loudness * one(*cut)
    return loudness


def noise(rng, dims, width, most, cuts=(), kind=jnp.bfloat16):
    values = width * jax.random.normal(rng, dims, jnp.float32)
    if cuts:
        values = values * block_levels(rng, dims, cuts, -0.22, 0.18)
    return jnp.clip(values, -most, most).astype(kind)


def bell_draw_with(key, shape, deviation, reach, cuts, heavy, kind=jnp.bfloat16):
    drawn = deviation * jax.random.normal(key, shape, jnp.float32)
    if cuts:
        drawn = drawn * block_levels(key, shape, cuts, -0.22, 0.18)
    return jnp.clip(strengthened(drawn, jax.random.fold_in(key, 3), *heavy), -reach, reach).astype(kind)


def setup_inputs(seed: int = 0) -> dict:
    splits = jax.random.split(jax.random.key(seed), 10)
    return {
        "hidden_in": noise(splits[0], (TOKENS, D), 1.0, 6.0, ((0, 32),)),
        "norm_gains": jnp.clip(1.0 + 0.18 * jax.random.normal(splits[1], (2, D), jnp.float32), 0.099609375, 1.8984375).astype(jnp.bfloat16),
        "w_qkv": noise(splits[2], (3 * D, D), D ** -0.5, 0.21875, ((0, 32),)),
        "w_attn_out": noise(splits[3], (D, D), (D // 64) ** -0.5, 1.75, ((0, 32),)),
        "w_in": noise(splits[4], (2 * FF, D), D ** -0.5, 0.21875, ((0, 32),)),
        "w_down": noise(splits[5], (D, FF), FF ** -0.5, 0.1875, ((0, 32),)),
        "cotangent": bell_draw_with(splits[6], (TOKENS, D), 1.0, 6.0, ((0, 32),), (0, 1, 32, 2.75)),
        "segment_ids": draw_segment_ids(jax.random.fold_in(splits[9], 71), 0),
        "row_counts": draw_row_counts(jax.random.fold_in(splits[9], 71), 0),
    }


EPS = 1e-05
THETA = 160000.0
NEG = -1e+30
HIGH = lax.Precision.HIGHEST

@jax.custom_vjp
def low(v):
    return lax.optimization_barrier(v.astype(jnp.bfloat16)).astype(jnp.float32)

@jax.custom_vjp
def low_back(v):
    return v

def low_keep(v):
    return (low(v), None)

def low_pass(kept, grad):
    return (grad,)

def back_keep(v):
    return (v, None)

def back_low(kept, grad):
    return (low(grad),)
low.defvjp(low_keep, low_pass)
low_back.defvjp(back_keep, back_low)

def layer_norm(row_values, gain):
    mean_value = lax.optimization_barrier(jnp.mean(row_values, axis=-1, keepdims=True))
    centred = row_values - mean_value
    variance = lax.optimization_barrier(jnp.mean(centred * centred, axis=-1, keepdims=True))
    return centred * lax.rsqrt(variance + EPS) * gain

def doc_positions(seg_ids):
    row_index = jnp.arange(seg_ids.shape[0], dtype=jnp.int32)
    begins = jnp.concatenate([jnp.ones((1,), dtype=jnp.bool_), seg_ids[1:] != seg_ids[:-1]])
    first_row = lax.cummax(jnp.where(begins, row_index, 0), axis=0)
    return (row_index - first_row).astype(jnp.float32)

def rotary_tables(position, head_size):
    half_size = head_size // 2
    freqs = THETA ** (-jnp.arange(half_size, dtype=jnp.float32) * 2.0 / head_size)
    angles = position[:, None] * freqs[None, :]
    angles = jnp.concatenate([angles, angles], axis=1)
    return (jnp.cos(angles), jnp.sin(angles))

def rotate(head_values, cos_table, sin_table):
    half_size = head_values.shape[-1] // 2
    turned = jnp.concatenate([-head_values[..., half_size:], head_values[..., :half_size]], axis=-1)
    return head_values * cos_table[:, None, :] + turned * sin_table[:, None, :]

def layer_block(start_rows, seg_ids, group_counts, params):
    gains, w_qkv, w_attn_out, w_in, w_down = params
    row_total = start_rows.shape[0]
    row_index = jnp.arange(row_total, dtype=jnp.int32)
    block_of_row = (row_index // TOK_DEV).astype(jnp.int32)
    valid = row_index % TOK_DEV < group_counts[block_of_row]
    keep_rows = valid.astype(start_rows.dtype)[:, None]
    normed1 = low(layer_norm(start_rows, gains[0]))
    qkv = low_back(jnp.dot(normed1, w_qkv.T, precision=HIGH))
    cos_table, sin_table = rotary_tables(doc_positions(seg_ids), HEAD_DIM)
    q_rot = low_back(low(rotate(qkv[:, :D].reshape(row_total, HEADS, HEAD_DIM), cos_table, sin_table)))
    k_rot = low_back(low(rotate(qkv[:, D:2 * D].reshape(row_total, HEADS, HEAD_DIM), cos_table, sin_table)))
    v_rot = low_back(low(qkv[:, 2 * D:].reshape(row_total, HEADS, HEAD_DIM)))
    scores = low_back(jnp.einsum('qhd,khd->hqk', q_rot, k_rot, precision=HIGH) * 0.125)
    same_doc = (seg_ids[:, None] == seg_ids[None, :]) & valid[:, None] & valid[None, :]
    allowed = same_doc | (row_index[:, None] == row_index[None, :])
    probs = low(jax.nn.softmax(jnp.where(allowed[None], scores, NEG), axis=-1))
    attended = jnp.einsum('hqk,khd->qhd', probs, v_rot, precision=HIGH).reshape(row_total, D)
    attended = low_back(low(attended))
    residual = start_rows + keep_rows * low_back(jnp.dot(attended, w_attn_out.T, precision=HIGH))
    normed2 = low(layer_norm(residual, gains[1]))
    both_parts = jnp.dot(normed2, w_in.T, precision=HIGH)
    gate = low_back(both_parts[:, :FF])
    up_part = low_back(both_parts[:, FF:])
    hidden = low(jax.nn.gelu(gate, approximate=False) * up_part)
    return residual + keep_rows * low_back(jnp.dot(hidden, w_down.T, precision=HIGH))

def reference(hidden_in, norm_gains, w_qkv, w_attn_out, w_in, w_down, cotangent, segment_ids, row_counts):
    group_rows = N_HD * TOK_DEV
    start_rows = hidden_in.astype(jnp.float32).reshape(N_TOK, group_rows, D)
    seg_groups = segment_ids.reshape(N_TOK, group_rows)
    count_groups = row_counts.reshape(N_TOK, N_HD)

    def forward(rows_all, gains_f, qkv_f, attn_out_f, in_f, down_f):
        params = (gains_f, qkv_f, attn_out_f, in_f, down_f)

        def one_group(item):
            return layer_block(item[0], item[1], item[2], params)
        return lax.map(jax.checkpoint(one_group), (rows_all, seg_groups, count_groups))
    result, pull_back = jax.vjp(forward, start_rows, norm_gains.astype(jnp.float32), w_qkv.astype(jnp.float32), w_attn_out.astype(jnp.float32), w_in.astype(jnp.float32), w_down.astype(jnp.float32))
    grads = pull_back(cotangent.astype(jnp.float32).reshape(N_TOK, group_rows, D))
    scale = 1.0 / math.sqrt(TOKENS)
    return (result.reshape(TOKENS, D).astype(jnp.bfloat16), grads[0].reshape(TOKENS, D).astype(jnp.bfloat16), grads[2] * scale, grads[3] * scale, grads[4] * scale, grads[5] * scale, grads[1] * scale)
```

```python
import functools
import math

import jax
import jax.numpy as jnp
import numpy as np
from jax import lax
from jax.experimental import pallas as pl
from jax.experimental.pallas import tpu as pltpu
from jax.sharding import PartitionSpec as P

HEADS = 12
HEAD_DIM = 64
EPS = 1e-05
THETA = 160000.0
NEG = -1e30
MESH = pl.DeviceIdType.MESH
F32 = jnp.float32
BF16 = jnp.bfloat16


def dot_nt(a, b):
    return lax.dot_general(a, b, (((1,), (1,)), ((), ())), preferred_element_type=F32)


def dot_nn(a, b):
    return lax.dot_general(a, b, (((1,), (0,)), ((), ())), preferred_element_type=F32)


def dot_tn(a, b):
    return lax.dot_general(a, b, (((0,), (0,)), ((), ())), preferred_element_type=F32)


def al(i, m):
    return pl.multiple_of(i, m)


def low_half(shape):
    lane = lax.broadcasted_iota(jnp.int32, shape, 1)
    return lane < HEAD_DIM


def rotated(u, cos, sin):
    lane = lax.broadcasted_iota(jnp.int32, cos.shape, 1)
    first = (lane % HEAD_DIM) < (HEAD_DIM // 2)
    parts = []
    for i in range(u.shape[1] // 128):
        s = u[:, i * 128 : (i + 1) * 128]
        swapped = jnp.where(first, pltpu.roll(s, 96, 1), pltpu.roll(s, 32, 1))
        parts.append(s * cos + swapped * sin)
    return parts[0] if len(parts) == 1 else jnp.concatenate(parts, axis=1)


def by_head(slab):
    lo = low_half(slab.shape)
    zero = jnp.zeros_like(slab)
    return jnp.where(lo, slab, zero), jnp.where(lo, zero, slab)


def norm_stats(u):
    mean = jnp.mean(u, axis=1, keepdims=True)
    centred = u - mean
    rstd = lax.rsqrt(jnp.mean(centred * centred, axis=1, keepdims=True) + EPS)
    return centred * rstd, rstd


def fold_rows(u):
    return jnp.sum(u.reshape(u.shape[0] // 8, 8, u.shape[1]), axis=0)


def layer_kernel(
    meta, x, cot, gains, wq, wo, wi, wd, freq,
    out, ingrad, gq, go, gi, gd, gg,
    x3, n1, cos_t, sin_t, krow, kcol, bias, q, k, v, p, att, res, n2, ga, gb, hid,
    cb, ggu, gres, gb1, gat, dkm, dsend, drecv, gqkv, gacc, pmeta,
    ssem, rsem,
):
    c = lax.axis_index("hd")
    half = x.shape[0] // 2
    rows = x.shape[0]
    d = x.shape[1]
    ff = wd.shape[1]
    so = al(c * half, half)
    mo = al((1 - c) * half, half)
    partner = {"hd": 1 - c}

    barrier = pltpu.get_barrier_semaphore()
    pl.semaphore_signal(barrier, inc=1, device_id=partner, device_id_type=MESH)
    pl.semaphore_wait(barrier, 1)

    def to_partner(src, dst, i):
        return pltpu.make_async_remote_copy(
            src, dst, ssem.at[i], rsem.at[i], device_id=partner, device_id_type=MESH
        )

    send_meta = to_partner(meta, pmeta, 0)
    send_x = to_partner(x.at[pl.ds(mo, half)], x3.at[pl.ds(2 * half, half)], 1)
    send_meta.start()
    send_x.start()
    x3[0:half] = x[pl.ds(so, half), :]
    x3[half : 2 * half] = x[pl.ds(mo, half), :]
    send_meta.wait()

    lane = lax.broadcasted_iota(jnp.int32, (1, half), 1)
    sets = ((meta, so, c * rows), (meta, mo, c * rows), (pmeta, so, (1 - c) * rows))
    for i, (ref, off, base) in enumerate(sets):
        cols = slice(i * half, (i + 1) * half)
        seg = ref[:, pl.ds(off, half)]
        local = lane + off
        grow = local + base
        valid = local < ref[0:1, rows : rows + 1]
        krow[0:1, cols] = jnp.where(valid, seg, -1 - grow).astype(F32)
        krow[1:2, cols] = seg.astype(F32)
        krow[2:3, cols] = grow.astype(F32)
        krow[3:8, cols] = jnp.broadcast_to(valid.astype(F32), (5, half))
    kcol[...] = krow[...].T

    def tables(i, _):
        r = pl.ds(al(i * 64, 64), 64)
        col = kcol[r, :]
        same = col[:, 1:2] == krow[1:2, :]
        start = jnp.min(jnp.where(same, krow[2:3, :], 1e9), axis=1, keepdims=True)
        angle = (col[:, 2:3] - start) * freq[0:1, :]
        cos_t[r, :] = jnp.cos(angle)
        sin_t[r, :] = jnp.sin(angle) * freq[1:2, :]
        return 0

    lax.fori_loop(0, 3 * half // 64, tables, 0)
    bias[:, 0:half] = jnp.where(kcol[0:half, 0:1] == krow[0:1, 0:half], 0.0, NEG)
    bias[:, half:] = jnp.where(kcol[half : 2 * half, 0:1] == krow[0:1, half:], 0.0, NEG)
    send_x.wait()

    def norm1(i, _):
        r = pl.ds(al(i * 128, 128), 128)
        n, _r = norm_stats(x3[r, :].astype(F32))
        n1[r, :] = (n * gains[0:1, :]).astype(BF16)
        return 0

    lax.fori_loop(0, 3 * half // 128, norm1, 0)

    def project(j, _):
        b = pl.ds(al(j * 256, 256), 256)
        u = dot_nt(n1[0:rows, :], wq[b, :])
        q[:, b] = (rotated(u, cos_t[0:rows, :], sin_t[0:rows, :]) * 0.125).astype(BF16)
        u = dot_nt(n1[...], wq[pl.ds(al(d + j * 256, 256), 256), :])
        k[:, b] = rotated(u, cos_t[...], sin_t[...]).astype(BF16)
        u = dot_nt(n1[...], wq[pl.ds(al(2 * d + j * 256, 256), 256), :])
        v[:, b] = u.astype(BF16)
        return 0

    lax.fori_loop(0, d // 256, project, 0)

    qs_, ks_ = (slice(0, half), slice(half, rows)), (slice(0, half), slice(half, 3 * half))

    def attend(hp, _):
        lanes = pl.ds(al(hp * 128, 128), 128)
        for qs, ks in zip(qs_, ks_):
            qh = by_head(q[qs, lanes])
            kk = k[ks, lanes]
            vh = by_head(v[ks, lanes])
            probs = []
            for h in range(2):
                s = dot_nt(qh[h], kk) + bias[:, ks]
                e = jnp.exp(s - jnp.max(s, axis=1, keepdims=True))
                e = (e * (1.0 / jnp.sum(e, axis=1, keepdims=True))).astype(BF16)
                p[2 * hp + h, :, ks] = e
                probs.append(e)
            o = dot_nn(jnp.concatenate(probs, axis=1), jnp.concatenate(vh, axis=0))
            att[qs, lanes] = o.astype(BF16)
        return 0

    lax.fori_loop(0, HEADS // 2, attend, 0)

    def after_attention(i, _):
        r = pl.ds(al(i * 256, 256), 256)
        u = x3[r, :].astype(F32) + kcol[r, 3:4] * dot_nt(att[r, :], wo[...])
        res[r, :] = u
        n, _r = norm_stats(u)
        n2[r, :] = (n * gains[1:2, :]).astype(BF16)
        return 0

    lax.fori_loop(0, rows // 256, after_attention, 0)

    def feed(j, _):
        b = pl.ds(al(j * 128, 128), 128)
        w = jnp.concatenate([wi[b, :], wi[pl.ds(al(ff + j * 128, 128), 128), :]], axis=0)
        u = dot_nt(n2[...], w)
        gate, up = u[:, :128], u[:, 128:]
        cdf = 0.5 * (1.0 + lax.erf(gate * (1.0 / math.sqrt(2.0))))
        pdf = jnp.exp(-0.5 * gate * gate) * (1.0 / math.sqrt(2.0 * math.pi))
        act = gate * cdf
        ga[:, b] = up * (cdf + gate * pdf)
        gb[:, b] = act
        hid[:, b] = (act * up).astype(BF16)
        return 0

    lax.fori_loop(0, ff // 128, feed, 0)

    for i, off in ((0, so), (1, mo)):
        r = slice(i * half, (i + 1) * half)
        cb[r, :] = (cot[pl.ds(off, half), :].astype(F32) * kcol[r, 3:4]).astype(BF16)

    def down(j, _):
        b = pl.ds(al(j * 256, 256), 256)
        y = (res[:, b] + kcol[0:rows, 3:4] * dot_nt(hid[...], wd[b, :])).astype(BF16)
        out[pl.ds(so, half), b] = y[:half]
        out[pl.ds(mo, half), b] = y[half:]
        return 0

    lax.fori_loop(0, d // 256, down, 0)

    def down_grad(j, _):
        b = pl.ds(al(j * 256, 256), 256)
        gd[b, :] = dot_tn(cb[:, b], hid[...]).astype(gd.dtype)
        return 0

    lax.fori_loop(0, d // 256, down_grad, 0)

    def hidden_grad(j, _):
        b = pl.ds(al(j * 384, 384), 384)
        u = dot_nn(cb[...], wd[:, b])
        ggu[:, b] = (u * ga[:, b]).astype(BF16)
        ggu[:, pl.ds(al(ff + j * 384, 384), 384)] = (u * gb[:, b]).astype(BF16)
        return 0

    lax.fori_loop(0, ff // 384, hidden_grad, 0)
    gacc[...] = jnp.zeros_like(gacc)

    def feed_back(i, _):
        r = pl.ds(al(i * 256, 256), 256)
        off = al(jnp.where(i == 0, so, mo), 256)
        g = dot_nn(ggu[r, :], wi[...])
        n, rstd = norm_stats(res[r, :])
        gacc[8:16, :] += fold_rows(g * n)
        g = g * gains[1:2, :]
        g = g - jnp.mean(g, axis=1, keepdims=True) - n * jnp.mean(g * n, axis=1, keepdims=True)
        g = cot[pl.ds(off, 256), :].astype(F32) + rstd * g
        gres[r, :] = g
        gb1[r, :] = (g * kcol[r, 3:4]).astype(BF16)
        return 0

    lax.fori_loop(0, rows // 256, feed_back, 0)

    def in_grad(j, _):
        b = pl.ds(al(j * 256, 256), 256)
        gi[b, :] = dot_tn(ggu[:, b], n2[...]).astype(gi.dtype)
        return 0

    lax.fori_loop(0, 2 * ff // 256, in_grad, 0)

    def out_grad(j, _):
        b = pl.ds(al(j * 256, 256), 256)
        go[b, :] = dot_tn(gb1[:, b], att[...]).astype(go.dtype)
        gat[:, b] = dot_nn(gb1[...], wo[:, b]).astype(BF16)
        return 0

    lax.fori_loop(0, d // 256, out_grad, 0)

    def attend_back(hp, qs, ks):
        lanes = pl.ds(al(hp * 128, 128), 128)
        do = gat[qs, lanes]
        doh = by_head(do)
        qh = by_head(q[qs, lanes])
        kh = by_head(k[ks, lanes])
        vv = v[ks, lanes]
        deltas = by_head(do.astype(F32) * att[qs, lanes].astype(F32))
        ds, ps = [], []
        for h in range(2):
            delta = jnp.sum(deltas[h], axis=1, keepdims=True)
            ph = p[2 * hp + h, :, ks]
            dp = dot_nt(doh[h], vv)
            ds.append((ph.astype(F32) * (dp - delta)).astype(BF16))
            ps.append(ph)
        dq = dot_nn(jnp.concatenate(ds, axis=1), jnp.concatenate(kh, axis=0)) * 0.125
        dk = dot_tn(jnp.concatenate(ds, axis=0), jnp.concatenate(qh, axis=0))
        dv = dot_tn(jnp.concatenate(ps, axis=0), jnp.concatenate(doh, axis=0))
        gqkv[qs, lanes] = rotated(dq, cos_t[qs, :], -sin_t[qs, :]).astype(BF16)
        return dk, dv

    def back_shared(hp, _):
        dk, dv = attend_back(hp, qs_[1], ks_[1])
        a, b = pl.ds(al(hp * 128, 128), 128), pl.ds(al(d + hp * 128, 128), 128)
        dkm[:, a] = dk[:half]
        dkm[:, b] = dv[:half]
        dsend[:, a] = dk[half:].astype(BF16)
        dsend[:, b] = dv[half:].astype(BF16)
        return 0

    lax.fori_loop(0, HEADS // 2, back_shared, 0)
    send_d = to_partner(dsend, drecv, 2)
    send_d.start()

    def back_solo(hp, _):
        dk, dv = attend_back(hp, qs_[0], ks_[0])
        a, b = pl.ds(al(d + hp * 128, 128), 128), pl.ds(al(2 * d + hp * 128, 128), 128)
        gqkv[0:half, a] = rotated(dk, cos_t[0:half, :], -sin_t[0:half, :]).astype(BF16)
        gqkv[0:half, b] = dv.astype(BF16)
        return 0

    lax.fori_loop(0, HEADS // 2, back_solo, 0)
    send_d.wait()

    def join(hp, _):
        a, b = pl.ds(al(hp * 128, 128), 128), pl.ds(al(d + hp * 128, 128), 128)
        e = pl.ds(al(2 * d + hp * 128, 128), 128)
        dk = dkm[:, a] + drecv[:, a].astype(F32)
        dv = dkm[:, b] + drecv[:, b].astype(F32)
        r = slice(half, rows)
        gqkv[r, b] = rotated(dk, cos_t[r, :], -sin_t[r, :]).astype(BF16)
        gqkv[r, e] = dv.astype(BF16)
        return 0

    lax.fori_loop(0, HEADS // 2, join, 0)

    def qkv_grad(j, _):
        b = pl.ds(al(j * 256, 256), 256)
        gq[b, :] = dot_tn(gqkv[:, b], n1[0:rows, :]).astype(gq.dtype)
        return 0

    lax.fori_loop(0, 3 * d // 256, qkv_grad, 0)

    def first_back(i, _):
        r = pl.ds(al(i * 256, 256), 256)
        off = al(jnp.where(i == 0, so, mo), 256)
        g = dot_nn(gqkv[r, :], wq[...])
        n, rstd = norm_stats(x3[r, :].astype(F32))
        gacc[0:8, :] += fold_rows(g * n)
        g = g * gains[0:1, :]
        g = g - jnp.mean(g, axis=1, keepdims=True) - n * jnp.mean(g * n, axis=1, keepdims=True)
        ingrad[pl.ds(off, 256), :] = (gres[r, :] + rstd * g).astype(BF16)
        return 0

    lax.fori_loop(0, rows // 256, first_back, 0)
    gg[0:1, :] = jnp.sum(gacc[0:8, :], axis=0, keepdims=True)
    gg[1:2, :] = jnp.sum(gacc[8:16, :], axis=0, keepdims=True)


def frequency_rows():
    w = np.arange(128) % HEAD_DIM
    f = np.float32(THETA) ** (-(w % 32).astype(np.float32) * 2.0 / HEAD_DIM)
    sign = np.where(w < 32, -1.0, 1.0)
    rows = np.zeros((8, 128), np.float32)
    rows[0], rows[1] = f, sign
    return rows


def per_device(
    hidden_in, norm_gains, w_qkv, w_attn_out, w_in, w_down, cotangent, segment_ids, row_counts
):
    both = ("tok", "hd")
    rows, d = hidden_in.shape
    ff = w_down.shape[1]
    half = rows // 2
    wq, wo, wi, wd = (
        lax.all_gather(w, both, axis=0, tiled=True) for w in (w_qkv, w_attn_out, w_in, w_down)
    )
    gains = lax.all_gather(norm_gains, both, axis=1, tiled=True).astype(F32)
    meta = jnp.concatenate([segment_ids, jnp.broadcast_to(row_counts, (128,))])[None]
    vmem = pl.BlockSpec(memory_space=pltpu.VMEM)
    V = pltpu.VMEM
    gdt = BF16
    outs = pl.pallas_call(
        layer_kernel,
        out_shape=[
            jax.ShapeDtypeStruct((rows, d), BF16),
            jax.ShapeDtypeStruct((rows, d), BF16),
            jax.ShapeDtypeStruct((3 * d, d), gdt),
            jax.ShapeDtypeStruct((d, d), gdt),
            jax.ShapeDtypeStruct((2 * ff, d), gdt),
            jax.ShapeDtypeStruct((d, ff), gdt),
            jax.ShapeDtypeStruct((2, d), F32),
        ],
        in_specs=[vmem] * 9,
        out_specs=[vmem] * 7,
        scratch_shapes=[
            V((3 * half, d), BF16),
            V((3 * half, d), BF16),
            V((3 * half, 128), F32),
            V((3 * half, 128), F32),
            V((8, 3 * half), F32),
            V((3 * half, 8), F32),
            V((half, 3 * half), F32),
            V((rows, d), BF16),
            V((3 * half, d), BF16),
            V((3 * half, d), BF16),
            V((HEADS, half, 3 * half), BF16),
            V((rows, d), BF16),
            V((rows, d), F32),
            V((rows, d), BF16),
            V((rows, ff), F32),
            V((rows, ff), F32),
            V((rows, ff), BF16),
            V((rows, d), BF16),
            V((rows, 2 * ff), BF16),
            V((rows, d), F32),
            V((rows, d), BF16),
            V((rows, d), BF16),
            V((half, 2 * d), F32),
            V((half, 2 * d), BF16),
            V((half, 2 * d), BF16),
            V((rows, 3 * d), BF16),
            V((16, d), F32),
            V(meta.shape, jnp.int32),
            pltpu.SemaphoreType.DMA((3,)),
            pltpu.SemaphoreType.DMA((3,)),
        ],
        compiler_params=pltpu.CompilerParams(
            collective_id=0, has_side_effects=True, vmem_limit_bytes=67043328
        ),
    )(meta, hidden_in, cotangent, gains, wq, wo, wi, wd, jnp.asarray(frequency_rows()))
    output, input_grad, gq, go, gi, gd, gg = outs
    total = rows * lax.axis_size("tok") * lax.axis_size("hd")
    scale = 1.0 / math.sqrt(total)
    sums = [
        lax.psum_scatter(g, both, scatter_dimension=0, tiled=True).astype(F32) * scale
        for g in (gq, go, gi, gd)
    ]
    sum_g = lax.psum_scatter(gg, both, scatter_dimension=1, tiled=True) * scale
    return (output, input_grad, *sums, sum_g)


def solution(mesh):
    both = ("tok", "hd")
    return jax.shard_map(
        per_device,
        mesh=mesh,
        in_specs=(
            P(both, None), P(None, both), P(both, None), P(both, None), P(both, None),
            P(both, None), P(both, None), P(both), P(both),
        ),
        out_specs=(
            P(both, None), P(both, None), P(both, None), P(both, None), P(both, None),
            P(both, None), P(None, both),
        ),
        check_vma=False,
    )
```
